256 devices in a mesh: sub: 32 (over y, z), crs: 8 (over x, core).
Axes of the slice: x: 4, y: 4, z: 8, core: 2. Of those that a mesh axis runs over, the one named last changes fastest.
Arguments:
- dual_ops: bfloat16 [384, 1536, 1536], P('sub', 'crs')
- rigid_traces: float32 [384, 6, 1536], P('sub'), may hold values from -0.625 to 0.625
- coarse_factor: float32 [2304, 2304], P('sub', 'crs')
- partner: int32 [384, 12], P('sub'), may hold values from -1 to 287, as said below
- send_list: int32 [64, 72], P('sub'), may hold values from -1 to 143, as said below
- mode_count: int32 [384], P('sub'), may hold values from 0 to 6
- dual_rhs: float32 [384, 1536], P('sub'), may hold values from -6 to 6
- rigid_load: float32 [2304], P('sub'), may hold values from -2400 to 2400
Outputs:
- multipliers: float32 [384, 1536], P('sub')
- projected_residual: float32 [384, 1536], P('sub')
The draws below stay inside these ranges and needn't reach their ends.
Inputs may be any that keep to these rules, and one draw needn't show every extreme that they name: For each block of a subdomain (subdomains in order, 12 blocks each): -1 for a padding block, else the position of its partner block in the list made of this index of sub's 12 * 12 blocks in order, then the 72 blocks received from the index before along sub, then the 72 from the index after. Partnership is mutual, never a block with itself, never across more than one index of sub. `send_list`: rows 2i and 2i+1 belong to index i of sub: its local blocks sent to the index before and to the index after, -1 in unused slots; the k-th block received from a neighbour is the k-th entry of that neighbour's row toward this index. The first index sends nothing before and the last nothing after; each boundary between neighbouring indices carries 72 // 2 to 72 blocks, one boundary exactly 72.
All inputs are finite; a program needn't handle non-finite values.
Results may differ from the reference program's by a relative error of at most 0.012.
The reference program's roundings to bfloat16 on the way count: a program that leaves them out, or rounds other values in their place, can miss the bound.
Values sent between devices are 32-bit elements; how exact they have to be, the bound alone decides.
A program may use at most 64 MiB of HBM per device.

```python
import math
import jax
import jax.numpy as jnp
from jax import lax

SUB_DEV = 12
BLOCKS = 12
BLOCK = 128
MODES = 6
ITERATIONS = 2
ORDER = 1536
SLOTS = 72
SUBDOMAINS = 384
COARSE = 2304
N_SUB = 32


def pairing(key):
    local_blocks = SUB_DEV * BLOCKS
    base_key = jax.random.fold_in(key, 7)
    count_key, pick_key, perm_key, local_key = jax.random.split(base_key, 4)
    crossing = jax.random.randint(count_key, (N_SUB - 1,), SLOTS // 2, SLOTS + 1)
    crossing = crossing.at[jax.random.randint(pick_key, (), 0, N_SUB - 1)].set(SLOTS)
    zero_one = jnp.zeros((1,), jnp.int32)
    left_count = jnp.concatenate([zero_one, crossing])
    right_count = jnp.concatenate([crossing, zero_one])
    perms = jax.vmap(lambda sub_key: jax.random.permutation(sub_key, local_blocks))(jax.random.split(perm_key, N_SUB))
    remain = local_blocks - left_count - right_count
    pair_count = jax.random.randint(local_key, (N_SUB,), remain // 4, remain // 2 + 1)
    position = jnp.arange(local_blocks, dtype=jnp.int32)[None, :]
    left_col = left_count[:, None]
    right_col = right_count[:, None]
    offset = position - left_col - right_col
    mate_pos = jnp.clip(left_col + right_col + jnp.bitwise_xor(jnp.maximum(offset, 0), 1), 0, local_blocks - 1)
    mate = jnp.take_along_axis(perms, mate_pos, axis=1)
    codes = jnp.where(position < left_col, local_blocks + position, jnp.where(position < left_col + right_col, local_blocks + SLOTS + position - left_col, jnp.where(offset < 2 * pair_count[:, None], mate, -1)))
    rows_idx = jnp.arange(N_SUB, dtype=jnp.int32)[:, None]
    partner_grid = jnp.zeros((N_SUB, local_blocks), jnp.int32).at[rows_idx, perms].set(codes.astype(jnp.int32))
    slot_idx = jnp.arange(SLOTS, dtype=jnp.int32)[None, :]
    to_before = jnp.where(slot_idx < left_col, perms[:, :SLOTS], -1)
    after_pos = jnp.clip(left_col + slot_idx, 0, local_blocks - 1)
    to_after = jnp.where(slot_idx < right_col, jnp.take_along_axis(perms, after_pos, axis=1), -1)
    sends = jnp.stack([to_before, to_after], axis=1).reshape(2 * N_SUB, SLOTS).astype(jnp.int32)
    return (partner_grid.reshape(SUB_DEV * N_SUB, BLOCKS), sends)


def draw_partner(key, part):
    return pairing(key)[0]


def draw_send_list(key, part):
    return pairing(key)[1]


def draw_dual_ops(key, part):
    order_len = BLOCKS * BLOCK

    def single(index):
        sub_key = jax.random.fold_in(jax.random.fold_in(key, 11), index)
        noise_key, diag_key = jax.random.split(sub_key)
        noise = jax.random.normal(noise_key, (order_len, order_len), jnp.float32)
        diagonal = jnp.exp(jax.random.uniform(diag_key, (order_len,), jnp.float32, math.log(1.5), math.log(4.0)))
        symmetric = (noise + noise.T) * (0.6 / math.sqrt(2.0 * order_len))
        return (symmetric + jnp.diag(diagonal)).astype(jnp.bfloat16)
    return lax.map(single, jnp.arange(SUB_DEV * N_SUB))


def draw_coarse_factor(key, part):
    coarse_len = MODES * SUB_DEV * N_SUB
    noise_key = jax.random.fold_in(key, 13)
    noise = jax.random.normal(noise_key, (coarse_len, coarse_len), jnp.float32)
    factor = 0.6 * jnp.eye(coarse_len, dtype=jnp.float32) + noise * (0.25 / math.sqrt(coarse_len))
    return 0.16 * factor


def touch_ends(values, key, low, high):
    longest = values.shape.index(max(values.shape))
    spots = []
    for shift in (0, 1):
        where = [jax.random.randint(jax.random.fold_in(key, axis), (), 0, length) for axis, length in enumerate(values.shape)]
        where[longest] = (where[longest] + shift) % values.shape[longest]
        spots.append(tuple(where))
    return values.at[spots[0]].set(low).at[spots[1]].set(high)


def block_levels(own_key, shape, shards, smallest, high):
    gain = 1.0
    for dim, blocks in shards:
        draws = jax.random.uniform(jax.random.fold_in(jax.random.fold_in(own_key, 6), dim), (blocks,), jnp.float32, smallest / len(shards), high / len(shards))
        gain = gain * jnp.repeat(jnp.exp(draws), shape[dim] // blocks).reshape((-1,) + (1,) * (len(shape) - 1 - dim))
    return gain


def scatter_about(key, dims, width, reach, shards=(), kind=jnp.bfloat16):
    drawn = jax.random.normal(key, dims, jnp.float32) * width
    if len(shards) > 0:
        drawn = block_levels(key, dims, shards, -0.22, 0.18) * drawn
    return jnp.clip(drawn, min=-reach, max=reach).astype(kind)


def setup_inputs(seed: int = 0) -> dict:
    key_list = jax.random.split(jax.random.key(seed), 9)
    dual_ops = draw_dual_ops(jax.random.fold_in(key_list[8], 71), 0)
    rigid_traces = scatter_about(key_list[1], (SUBDOMAINS, MODES, ORDER), (ORDER // 16) ** -0.5, 0.625, ((0, 32),), jnp.float32)
    coarse_factor = draw_coarse_factor(jax.random.fold_in(key_list[8], 71), 0)
    partner = draw_partner(jax.random.fold_in(key_list[8], 71), 0)
    send_list = draw_send_list(jax.random.fold_in(key_list[8], 71), 0)
    mode_count = touch_ends(jax.random.randint(key_list[5], (SUBDOMAINS,), 0, 7), jax.random.fold_in(key_list[5], 1), 0, 6).astype(jnp.int32)
    dual_rhs = scatter_about(key_list[6], (SUBDOMAINS, ORDER), 1.0, 6.0, ((0, 32),), jnp.float32)
    rigid_load = scatter_about(key_list[7], (COARSE,), 400.0, 2400.0, ((0, 32),), jnp.float32)
    return {"dual_ops": dual_ops, "rigid_traces": rigid_traces, "coarse_factor": coarse_factor, "partner": partner, "send_list": send_list, "mode_count": mode_count, "dual_rhs": dual_rhs, "rigid_load": rigid_load}


def reference(dual_ops, rigid_traces, coarse_factor, partner, send_list, mode_count, dual_rhs, rigid_load):
    local_blocks = SUB_DEV * BLOCKS
    codes_grid = partner.reshape(N_SUB, local_blocks)
    outgoing = send_list.reshape(N_SUB, 2, SLOTS)
    devices = jnp.arange(N_SUB, dtype=jnp.int32)[:, None]
    prev_dev = jnp.maximum(devices - 1, 0)
    next_dev = jnp.minimum(devices + 1, N_SUB - 1)
    left_slot = jnp.clip(codes_grid - local_blocks, 0, SLOTS - 1)
    right_slot = jnp.clip(codes_grid - local_blocks - SLOTS, 0, SLOTS - 1)
    from_before = prev_dev * local_blocks + jnp.maximum(outgoing[prev_dev, 1, left_slot], 0)
    from_after = next_dev * local_blocks + jnp.maximum(outgoing[next_dev, 0, right_slot], 0)
    own_block = devices * local_blocks + jnp.maximum(codes_grid, 0)
    target = jnp.where(codes_grid < local_blocks, own_block,
                       jnp.where(codes_grid < local_blocks + SLOTS, from_before, from_after)).reshape(-1)
    linked = (partner.reshape(-1) >= 0)[:, None]
    mode_mask = (jnp.arange(MODES, dtype=jnp.int32)[None, :] < mode_count[:, None]).astype(jnp.float32)

    def jump(vector):
        pieces = vector.reshape(-1, BLOCK)
        return jnp.where(linked, pieces - pieces[target], 0.0).reshape(vector.shape)

    def operator(vector):
        lowered = jump(vector).astype(jnp.bfloat16)

        def single(couple):
            return jnp.dot(couple[0], couple[1], preferred_element_type=jnp.float32)

        rows_out = lax.map(single, (dual_ops, lowered))
        return jump(rows_out)

    def restrict(vector):
        traced = jnp.einsum("skm,sm->sk", rigid_traces, jump(vector), precision=lax.Precision.HIGHEST) * mode_mask
        return traced.reshape(-1)

    def expand(coarse_vec):
        spread = jnp.einsum("skm,sk->sm", rigid_traces, coarse_vec.reshape(-1, MODES) * mode_mask,
                            precision=lax.Precision.HIGHEST)
        return jump(spread)

    def coarse(restricted):
        columns = jnp.dot(restricted, coarse_factor, precision=lax.Precision.HIGHEST)
        return jnp.dot(coarse_factor, columns, precision=lax.Precision.HIGHEST)

    def project(residual):
        projected = residual - expand(coarse(restrict(residual)))
        return projected, jnp.sum(residual * projected)

    multipliers = expand(coarse(rigid_load * mode_mask.reshape(-1)))
    residual = dual_rhs - operator(multipliers)
    projected, inner_rw = project(residual)
    direction = projected
    for turn_idx in range(ITERATIONS):
        applied = operator(direction)
        step_len = inner_rw / jnp.sum(direction * applied)
        multipliers = multipliers + step_len * direction
        residual = residual - step_len * applied
        projected, next_rw = project(residual)
        direction = projected + (next_rw / inner_rw) * direction
        inner_rw = next_rw
    return multipliers, projected
```

```python
import functools

import jax
import jax.numpy as jnp
from jax import lax
from jax.experimental import pallas as pl
from jax.experimental.pallas import tpu as pltpu
from jax.sharding import PartitionSpec as P

ITERATIONS = 2
LANES = 128
F32 = jnp.float32


def lane_sum(a):
    return jnp.sum(a, axis=1, keepdims=True)


def total(a):
    return jnp.sum(lane_sum(a), axis=0, keepdims=True)


def kernel(
    n_sub, n_crs,
    partner, sends, modes, load, ops_hbm, traces, factor, rhs,
    out_m, out_p,
    ops, tk, wk, gather, mate, res, jres, way, jway,
    cmsg, crecv, xmsg, xrecv, qmsg, qrecv, hmsg, hrecv,
    ops_sem, c_send, c_recv, x_send, x_recv, q_send, q_recv, h_send, h_recv,
):
    n_s, n_row, order = ops.shape
    n_b = order // LANES
    n_local = n_s * n_b
    n_k = tk.shape[0]
    n_col = factor.shape[1]
    slots = sends.shape[1]
    sub = lax.axis_index("sub")
    crs = lax.axis_index("crs")

    fetch = pltpu.make_async_copy(ops_hbm, ops, ops_sem)
    fetch.start()

    barrier = pltpu.get_barrier_semaphore()

    def greet(axis, me, count):
        def one(t, carry):
            pl.semaphore_signal(
                barrier, inc=1, device_id={axis: lax.rem(me + t, count)},
                device_id_type=pl.DeviceIdType.MESH,
            )
            return carry
        lax.fori_loop(1, count, one, 0)

    greet("sub", sub, n_sub)
    greet("crs", crs, n_crs)

    def copy(src, dst, send, recv, where):
        return pltpu.make_async_remote_copy(
            src_ref=src, dst_ref=dst, send_sem=send, recv_sem=recv,
            device_id=where, device_id_type=pl.DeviceIdType.MESH,
        )

    def spread(msg, slots_ref, send, recv, axis, me, count):
        def one(t, carry):
            copy(msg, slots_ref.at[t - 1], send, recv, {axis: lax.rem(me + t, count)}).start()
            return carry
        lax.fori_loop(1, count, one, 0)

    def arrivals(slots_ref, send, recv, axis, me, count):
        whole = slots_ref.at[pl.ds(0, count - 1)]
        return copy(whole, whole, send, recv, {axis: lax.rem(me + 1, count)})

    def slot_of(who, me, count):
        return lax.rem(me - who - 1 + count, count)

    def jump_start(v, j):
        for b in range(n_b):
            gather[pl.ds(b, n_s, stride=n_b), :] = v[:, b * LANES:(b + 1) * LANES]

        def pick(n, carry):
            for side in range(2):
                for m in range(8):
                    at = jnp.maximum(sends[side, n * 8 + m], 0)
                    hmsg[j, side, pl.ds(n * 8 + m, 1), :] = gather[pl.ds(at, 1), :]
            return carry
        lax.fori_loop(0, slots // 8, pick, 0)
        for side in range(2):
            there = lax.rem(sub + (n_sub - 1 if side == 0 else 1), n_sub)
            copy(hmsg.at[j, side], hrecv.at[j, 1 - side], h_send.at[j, side], h_recv.at[j, 1 - side],
                 {"sub": there}).start()

    def jump_end(v, j):
        for side in range(2):
            there = lax.rem(sub + 1, n_sub)
            copy(hmsg.at[j, side], hrecv.at[j, side], h_send.at[j, side], h_recv.at[j, side],
                 {"sub": there}).wait_recv()
            gather[pl.ds(n_local + side * slots, slots), :] = hrecv[j, side]

        def pair(s, carry):
            for b in range(n_b):
                code = partner[s, b]
                at = jnp.where(code < 0, s * n_b + b, code)
                mate[pl.ds(s * n_b + b, 1), :] = gather[pl.ds(at, 1), :]
            return carry
        lax.fori_loop(0, n_s, pair, 0)
        parts = [mate[pl.ds(b, n_s, stride=n_b), :] for b in range(n_b)]
        return v - jnp.concatenate(parts, axis=1)

    def pad_col(col):
        parts = []
        for n in range(3):
            piece = col[:, n * LANES:min((n + 1) * LANES, n_col)]
            if piece.shape[1] < LANES:
                piece = jnp.concatenate([piece, jnp.zeros((1, LANES - piece.shape[1]), F32)], axis=1)
            parts.append(piece)
        return parts

    lane = lax.broadcasted_iota(jnp.int32, (1, LANES), 1)

    def sub_start(n, col, scalars):
        for at, piece in enumerate(pad_col(col)):
            cmsg[n, at:at + 1, :] = piece
        last = jnp.zeros((1, LANES), F32)
        for at, value in enumerate(scalars):
            last = jnp.where(lane == at, value, last)
        cmsg[n, 3:4, :] = last
        crecv[n, n_sub - 1] = cmsg[n]
        spread(cmsg.at[n], crecv.at[n], c_send.at[n], c_recv.at[n], "sub", sub, n_sub)

    def sub_end(n):
        arrivals(crecv.at[n], c_send.at[n], c_recv.at[n], "sub", sub, n_sub).wait_recv()
        got = [crecv[n, slot_of(who, sub, n_sub)] for who in range(n_sub)]
        while len(got) > 1:
            got = [got[i] + got[i + 1] for i in range(0, len(got), 2)]
        tot = got[0]
        col = jnp.concatenate([tot[0:1], tot[1:2], tot[2:3, :n_col - 2 * LANES]], axis=1)
        return col, tot[3:4]

    wide = lax.broadcasted_iota(jnp.int32, (n_s, LANES), 1)
    tall = lax.broadcasted_iota(jnp.int32, (n_s, LANES), 0)

    def back(n, col):
        mix = jnp.zeros((n_s, LANES), F32)
        for k in range(n_k):
            mix = jnp.where(wide == k, lane_sum(wk[k] * col), mix)
        folded = lane_sum(col * col)
        mix = jnp.where((wide == n_k) & (tall == 0), folded, mix)
        xmsg[n] = mix
        xrecv[n, n_crs - 1] = mix
        spread(xmsg.at[n], xrecv.at[n], x_send.at[n], x_recv.at[n], "crs", crs, n_crs)

    def back_end(n):
        arrivals(xrecv.at[n], x_send.at[n], x_recv.at[n], "crs", crs, n_crs).wait_recv()
        tot = xrecv[n, slot_of(0, crs, n_crs)]
        for who in range(1, n_crs):
            tot = tot + xrecv[n, slot_of(who, crs, n_crs)]
        return tot

    def expand(tot, j):
        z = tk[0] * tot[:, 0:1]
        for k in range(1, n_k):
            z = z + tk[k] * tot[:, k:k + 1]
        jump_start(z, j)
        return jump_end(z, j)

    def restrict_col(jv):
        acc = None
        for k in range(n_k):
            e = lane_sum(tk[k] * jv)
            term = wk[k] * e
            acc = term if acc is None else acc + term
        return jnp.sum(acc, axis=0, keepdims=True)

    odd = lax.rem(crs, 2) == 1

    def operator(ju, n, j):
        row = lax.broadcasted_iota(jnp.int32, ju.shape, 0)
        acc = jnp.zeros((n_s, n_row), F32)
        for s in range(n_s):
            u = jnp.where(row == s, ju, 0.0).astype(jnp.bfloat16)
            acc = acc + lax.dot_general(u, ops[s], (((1,), (1,)), ((), ())), preferred_element_type=F32)
        blank = jnp.zeros((n_s, 2 * LANES - n_row), F32)
        lined = jnp.where(odd, jnp.concatenate([blank, acc], axis=1), jnp.concatenate([acc, blank], axis=1))
        for half in range(2):
            piece = lined[:, half * LANES:(half + 1) * LANES]
            qmsg[n, half] = piece
            qrecv[n, n_crs - 1, half] = piece
        spread(qmsg.at[n], qrecv.at[n], q_send.at[n], q_recv.at[n], "crs", crs, n_crs)
        arrivals(qrecv.at[n], q_send.at[n], q_recv.at[n], "crs", crs, n_crs).wait_recv()
        blocks = []
        for pair in range(n_crs // 2):
            even, uneven = slot_of(2 * pair, crs, n_crs), slot_of(2 * pair + 1, crs, n_crs)
            blocks.append(qrecv[n, even, 0])
            blocks.append(jnp.where(wide < LANES // 2, qrecv[n, even, 1], qrecv[n, uneven, 0]))
            blocks.append(qrecv[n, uneven, 1])
        q = jnp.concatenate(blocks, axis=1)
        jump_start(q, j)
        return jump_end(q, j)

    for s in range(n_s):
        for k in range(n_k):
            keep = jnp.where(k < modes[s], 1.0, 0.0).astype(F32)
            tk[k, s:s + 1, :] = traces[s, k:k + 1, :] * keep
            wk[k, s:s + 1, :] = factor[s * n_k + k:s * n_k + k + 1, :]
    col = jnp.zeros((1, n_col), F32)
    for s in range(n_s):
        for k in range(n_k):
            keep = jnp.where(k < modes[s], load[s * n_k + k], 0.0)
            col = col + factor[s * n_k + k:s * n_k + k + 1, :] * keep

    pl.semaphore_wait(barrier, n_sub - 1 + n_crs - 1)

    sub_start(0, col, ())
    jump_start(rhs, 0)
    jrhs = jump_end(rhs[...], 0)
    jres[...] = jrhs
    col, _ = sub_end(0)
    back(0, col)
    fetch.wait()
    mult = expand(back_end(0), 1)
    out_m[...] = mult
    applied = operator(2.0 * mult, 0, 2)
    r = rhs[...] - applied
    jr = jres[...] - 2.0 * applied
    res[...] = r
    jres[...] = jr
    sub_start(1, restrict_col(jr), (total(r * r),))
    col, tail = sub_end(1)
    square = tail[:, 0:1]
    back(1, col)
    tot = back_end(1)
    rw = square - tot[0:1, n_k:n_k + 1]
    lifted = expand(tot, 3)
    way[...] = res[...] - lifted
    jway[...] = jres[...] - 2.0 * lifted
    for turn in range(ITERATIONS):
        applied = operator(jway[...], 1 + turn, 4 + 2 * turn)
        d, r = way[...], res[...]
        sub_start(2 + turn, restrict_col(2.0 * applied),
                  (total(d * applied), total(r * applied), total(applied * applied)))
        change, tail = sub_end(2 + turn)
        alpha = rw / tail[:, 0:1]
        col = col - alpha * change
        back(2 + turn, col)
        square = square - 2.0 * alpha * tail[:, 1:2] + alpha * alpha * tail[:, 2:3]
        r = res[...] - alpha * applied
        jr = jres[...] - 2.0 * alpha * applied
        res[...] = r
        jres[...] = jr
        out_m[...] = out_m[...] + alpha * way[...]
        tot = back_end(2 + turn)
        lifted = expand(tot, 5 + 2 * turn)
        if turn == ITERATIONS - 1:
            out_p[...] = res[...] - lifted
        else:
            following = square - tot[0:1, n_k:n_k + 1]
            beta = following / rw
            way[...] = res[...] - lifted + beta * way[...]
            jway[...] = jres[...] - 2.0 * lifted + beta * jway[...]
            rw = following

    for n in range(ITERATIONS + 2):
        arrivals(crecv.at[n], c_send.at[n], c_recv.at[n], "sub", sub, n_sub).wait_send()
        arrivals(xrecv.at[n], x_send.at[n], x_recv.at[n], "crs", crs, n_crs).wait_send()
    for n in range(ITERATIONS + 1):
        arrivals(qrecv.at[n], q_send.at[n], q_recv.at[n], "crs", crs, n_crs).wait_send()
    for j in range(2 * ITERATIONS + 4):
        for side in range(2):
            copy(hmsg.at[j, side], hrecv.at[j, side], h_send.at[j, side], h_recv.at[j, side],
                 {"sub": lax.rem(sub + 1, n_sub)}).wait_send()


def local(n_sub, n_crs, ops, traces, factor, partner, sends, modes, rhs, load):
    n_s, n_row, order = ops.shape
    n_k = traces.shape[1]
    n_col = factor.shape[1]
    slots = sends.shape[1]
    n_local = n_s * order // LANES
    n_c, n_q, n_j = ITERATIONS + 2, ITERATIONS + 1, 2 * ITERATIONS + 4
    smem = pl.BlockSpec(memory_space=pltpu.SMEM)
    vmem = pl.BlockSpec(memory_space=pltpu.VMEM)
    dma = pltpu.SemaphoreType.DMA
    vector = (n_s, order)
    return pl.pallas_call(
        functools.partial(kernel, n_sub, n_crs),
        out_shape=(jax.ShapeDtypeStruct(vector, F32), jax.ShapeDtypeStruct(vector, F32)),
        in_specs=[smem, smem, smem, smem, pl.BlockSpec(memory_space=pl.ANY), vmem, vmem, vmem],
        out_specs=(vmem, vmem),
        scratch_shapes=[
            pltpu.VMEM(ops.shape, ops.dtype),
            pltpu.VMEM((n_k, n_s, order), F32),
            pltpu.VMEM((n_k, n_s, n_col), F32),
            pltpu.VMEM((n_local + 2 * slots, LANES), F32),
            pltpu.VMEM((n_local, LANES), F32),
            pltpu.VMEM(vector, F32),
            pltpu.VMEM(vector, F32),
            pltpu.VMEM(vector, F32),
            pltpu.VMEM(vector, F32),
            pltpu.VMEM((n_c, 4, LANES), F32),
            pltpu.VMEM((n_c, n_sub, 4, LANES), F32),
            pltpu.VMEM((n_c, n_s, LANES), F32),
            pltpu.VMEM((n_c, n_crs, n_s, LANES), F32),
            pltpu.VMEM((n_q, 2, n_s, LANES), F32),
            pltpu.VMEM((n_q, n_crs, 2, n_s, LANES), F32),
            pltpu.VMEM((n_j, 2, slots, LANES), F32),
            pltpu.VMEM((n_j, 2, slots, LANES), F32),
            dma, dma((n_c,)), dma((n_c,)), dma((n_c,)), dma((n_c,)), dma((n_q,)), dma((n_q,)),
            dma((n_j, 2)), dma((n_j, 2)),
        ],
        compiler_params=pltpu.CompilerParams(
            collective_id=0, has_side_effects=True, vmem_limit_bytes=48 * 1024 * 1024
        ),
    )(partner, sends, modes, load, ops, traces, factor, rhs)


def solution(mesh):
    return jax.shard_map(
        functools.partial(local, mesh.shape["sub"], mesh.shape["crs"]),
        mesh=mesh,
        in_specs=(
            P("sub", "crs", None),
            P("sub", None, None),
            P("sub", "crs"),
            P("sub", None),
            P("sub", None),
            P("sub"),
            P("sub", None),
            P("sub"),
        ),
        out_specs=(P("sub", None), P("sub", None)),
        check_vma=False,
    )
```

```python
import functools

import jax
import jax.numpy as jnp
from jax import lax
from jax.experimental import pallas as pl
from jax.experimental.pallas import tpu as pltpu
from jax.sharding import PartitionSpec as P

ITERATIONS = 2
LANES = 128
F32 = jnp.float32


def lane_sum(a):
    return jnp.sum(a, axis=1, keepdims=True)


def total(a):
    return jnp.sum(lane_sum(a), axis=0, keepdims=True)


def kernel(
    n_sub, n_crs,
    partner_in, sends_in, modes_in, load_in, ops_in, traces_in, factor_in, rhs_in,
    out_m, out_p,
    partner, sends, modes, load, ops, traces, factor, rhs,
    tk, tl, tp, wk, planes, mates, member, member_t, inner, gather, mate, lift, qv, res, jres, way, jway,
    cmsg, crecv, xmsg, xrecv, qmsg, qrecv, hmsg, hrecv, tmsg, trecv, wrecv, rmsg, rrecv,
    in_sem, c_send, c_recv, x_send, x_recv, q_send, q_recv, h_send, h_recv, t_send, t_recv, w_send, w_recv,
    r_send, r_recv,
):
    n_s, n_row, order = ops.shape
    n_b = order // LANES
    n_local = n_s * n_b
    n_k = tk.shape[0]
    n_col = factor.shape[1]
    slots = sends.shape[1]
    tile = 16
    sub = lax.axis_index("sub")
    crs = lax.axis_index("crs")

    pairs = ((partner_in, partner), (sends_in, sends), (modes_in, modes), (load_in, load),
             (factor_in, factor), (traces_in, traces), (rhs_in, rhs), (ops_in, ops))
    fetch = [pltpu.make_async_copy(a, b, in_sem.at[n]) for n, (a, b) in enumerate(pairs)]
    for one in fetch:
        one.start()

    barrier = pltpu.get_barrier_semaphore()

    def greet(axis, me, count):
        def one(t, carry):
            pl.semaphore_signal(
                barrier, inc=1, device_id={axis: lax.rem(me + t, count)},
                device_id_type=pl.DeviceIdType.MESH,
            )
            return carry
        lax.fori_loop(1, count, one, 0)

    greet("sub", sub, n_sub)
    greet("crs", crs, n_crs)

    def copy(src, dst, send, recv, where):
        return pltpu.make_async_remote_copy(
            src_ref=src, dst_ref=dst, send_sem=send, recv_sem=recv,
            device_id=where, device_id_type=pl.DeviceIdType.MESH,
        )

    def spread(msg, slots_ref, send, recv, axis, me, count):
        def one(t, carry):
            copy(msg, slots_ref.at[t - 1], send, recv, {axis: lax.rem(me + t, count)}).start()
            return carry
        lax.fori_loop(1, count, one, 0)

    def arrivals(slots_ref, send, recv, axis, me, count):
        whole = slots_ref.at[pl.ds(0, count - 1)]
        return copy(whole, whole, send, recv, {axis: lax.rem(me + 1, count)})

    def slot_of(who, me, count):
        return lax.rem(me - who - 1 + count, count)

    before, after = lax.rem(sub + n_sub - 1, n_sub), lax.rem(sub + 1, n_sub)

    def both(msg, recv_ref, send, recv):
        return [copy(msg[0], recv_ref.at[1], send.at[0], recv.at[1], {"sub": before}),
                copy(msg[1], recv_ref.at[0], send.at[1], recv.at[0], {"sub": after})]

    def rows_of(v, b):
        return v[:, b * LANES:(b + 1) * LANES]

    def jump_start(v, j):
        for b in range(n_b):
            gather[pl.ds(b, n_s, stride=n_b), :] = rows_of(v, b)

        def pick(n, carry):
            for side in range(2):
                for m in range(8):
                    at = jnp.maximum(sends[side, n * 8 + m], 0)
                    hmsg[j, side, pl.ds(n * 8 + m, 1), :] = gather[pl.ds(at, 1), :]
            return carry
        lax.fori_loop(0, slots // 8, pick, 0)

    def jump_copies(j):
        return both((hmsg.at[j, 0], hmsg.at[j, 1]), hrecv.at[j], h_send.at[j], h_recv.at[j])

    def jump_end(v, j):
        one, two = jump_copies(j)
        one.wait_recv()
        two.wait_recv()
        for side in range(2):
            gather[pl.ds(n_local + side * slots, slots), :] = hrecv[j, side]

        def pair(s, carry):
            for b in range(n_b):
                code = partner[s, b]
                at = jnp.where(code < 0, s * n_b + b, code)
                mate[pl.ds(s * n_b + b, 1), :] = gather[pl.ds(at, 1), :]
            return carry
        lax.fori_loop(0, n_s, pair, 0)
        parts = [mate[pl.ds(b, n_s, stride=n_b), :] for b in range(n_b)]
        return v - jnp.concatenate(parts, axis=1)

    lane = lax.broadcasted_iota(jnp.int32, (1, LANES), 1)
    wide = lax.broadcasted_iota(jnp.int32, (n_s, LANES), 1)

    def sub_start(n, col, scalars):
        for at in range(3):
            piece = col[:, at * LANES:min((at + 1) * LANES, n_col)]
            if piece.shape[1] < LANES:
                piece = jnp.concatenate([piece, jnp.zeros((1, LANES - piece.shape[1]), F32)], axis=1)
            cmsg[n, at:at + 1, :] = piece
        last = jnp.zeros((1, LANES), F32)
        for at, value in enumerate(scalars):
            last = jnp.where(lane == at, value, last)
        cmsg[n, 3:4, :] = last
        crecv[n, n_sub - 1] = cmsg[n]
        spread(cmsg.at[n], crecv.at[n], c_send.at[n], c_recv.at[n], "sub", sub, n_sub)

    def tree(got):
        while len(got) > 1:
            got = [got[i] + got[i + 1] for i in range(0, len(got), 2)]
        return got[0]

    def sub_end(n):
        arrivals(crecv.at[n], c_send.at[n], c_recv.at[n], "sub", sub, n_sub).wait_recv()
        tot = tree([crecv[n, slot_of(who, sub, n_sub)] for who in range(n_sub)])
        col = jnp.concatenate([tot[0:1], tot[1:2], tot[2:3, :n_col - 2 * LANES]], axis=1)
        return col, tot[3:4]

    def square_start(n, v):
        line = jnp.where(lane == 0, total(v * v), 0.0)
        rmsg[n] = line
        rrecv[n, n_sub - 1] = line
        spread(rmsg.at[n], rrecv.at[n], r_send.at[n], r_recv.at[n], "sub", sub, n_sub)

    def square_end(n):
        arrivals(rrecv.at[n], r_send.at[n], r_recv.at[n], "sub", sub, n_sub).wait_recv()
        return tree([rrecv[n, slot_of(who, sub, n_sub)] for who in range(n_sub)])[:, 0:1]

    n_x = 3 * n_k
    fold_at = 2 * n_x + 4

    def back(n, col):
        mix = jnp.zeros((n_s, LANES), F32)
        for near in range(3):
            for k in range(n_k):
                mix = jnp.where(wide == near * n_k + k, lane_sum(wk[near, k] * col), mix)
        low = jnp.concatenate([mix[8:n_s], jnp.zeros((16 - n_s, LANES), F32)], axis=0)
        msg = mix[0:8] + pltpu.roll(low, n_x, 1)
        at = (lax.broadcasted_iota(jnp.int32, (8, LANES), 1) == fold_at) & (
            lax.broadcasted_iota(jnp.int32, (8, LANES), 0) == 0)
        msg = jnp.where(at, lane_sum(col * col), msg)
        xmsg[n] = msg
        xrecv[n, n_crs - 1] = msg
        spread(xmsg.at[n], xrecv.at[n], x_send.at[n], x_recv.at[n], "crs", crs, n_crs)

    def back_end(n):
        arrivals(xrecv.at[n], x_send.at[n], x_recv.at[n], "crs", crs, n_crs).wait_recv()
        tot = tree([xrecv[n, slot_of(who, crs, n_crs)] for who in range(n_crs)])
        low = pltpu.roll(tot, LANES - n_x, 1)
        return jnp.concatenate([tot, low[:n_s - 8]], axis=0), tot[0:1, fold_at:fold_at + 1]

    def expand(mix):
        spare = jnp.zeros((tile - n_s, LANES), F32)
        rows = []
        for near in range(3):
            rows += [pltpu.roll(mix, LANES - near * n_k, 1) if near else mix, spare]
        rows.append(jnp.zeros((LANES - 3 * tile, LANES), F32))
        mates_x = jnp.dot(member[...], jnp.concatenate(rows, axis=0), precision=lax.Precision.HIGHEST,
                          preferred_element_type=F32)
        own = [mix[:, n_k + k:n_k + k + 1] for k in range(n_k)]
        for b in range(n_b):
            theirs = mates_x[b * tile:b * tile + n_s]
            acc = None
            for k in range(n_k):
                term = rows_of(tl[k], b) * own[k] - rows_of(tp[k], b) * theirs[:, k:k + 1]
                acc = term if acc is None else acc + term
            lift[:, b * LANES:(b + 1) * LANES] = acc

    def restrict_col(jv):
        acc = None
        for k in range(n_k):
            term = wk[1, k] * lane_sum(tl[k] * jv)
            acc = term if acc is None else acc + term
        return jnp.sum(acc, axis=0, keepdims=True)

    def adjoint_col(q):
        for b in range(n_b):
            line = jnp.zeros((n_s, LANES), F32)
            for k in range(n_k):
                line = jnp.where(wide == k, lane_sum(rows_of(tp[k], b) * rows_of(q, b)), line)
            inner[b * tile:b * tile + n_s, :] = line
        away = jnp.dot(member_t[...], inner[...], precision=lax.Precision.HIGHEST, preferred_element_type=F32)
        acc = None
        for k in range(n_k):
            for near in range(3):
                weight = -away[near * tile:near * tile + n_s, k:k + 1]
                if near == 1:
                    weight = weight + lane_sum(tl[k] * q)
                term = wk[near, k] * weight
                acc = term if acc is None else acc + term
        return jnp.sum(acc, axis=0, keepdims=True)

    odd = lax.rem(crs, 2) == 1

    def multiply(ju, n):
        row = lax.broadcasted_iota(jnp.int32, ju.shape, 0)
        acc = jnp.zeros((n_s, n_row), F32)
        for s in range(n_s):
            u = jnp.where(row == s, ju, 0.0).astype(jnp.bfloat16)
            acc = acc + lax.dot_general(u, ops[s], (((1,), (1,)), ((), ())), preferred_element_type=F32)
        blank = jnp.zeros((n_s, 2 * LANES - n_row), F32)
        lined = jnp.where(odd, jnp.concatenate([blank, acc], axis=1), jnp.concatenate([acc, blank], axis=1))
        for half in range(2):
            piece = rows_of(lined, half)
            qmsg[n, half] = piece
            qrecv[n, n_crs - 1, half] = piece
        spread(qmsg.at[n], qrecv.at[n], q_send.at[n], q_recv.at[n], "crs", crs, n_crs)
        arrivals(qrecv.at[n], q_send.at[n], q_recv.at[n], "crs", crs, n_crs).wait_recv()
        for pair in range(n_crs // 2):
            even, uneven = slot_of(2 * pair, crs, n_crs), slot_of(2 * pair + 1, crs, n_crs)
            at = 3 * pair * LANES
            qv[:, at:at + LANES] = qrecv[n, even, 0]
            qv[:, at + LANES:at + 2 * LANES] = jnp.where(wide < LANES // 2, qrecv[n, even, 1], qrecv[n, uneven, 0])
            qv[:, at + 2 * LANES:at + 3 * LANES] = qrecv[n, uneven, 1]

    for one in fetch[:5]:
        one.wait()
    col = jnp.zeros((1, n_col), F32)
    for s in range(n_s):
        for k in range(n_k):
            keep = jnp.where(k < modes[s], load[s * n_k + k], 0.0)
            line = factor[s * n_k + k:s * n_k + k + 1, :]
            wk[1, k, s:s + 1, :] = line
            col = col + line * keep
    fetch[5].wait()
    for s in range(n_s):
        for k in range(n_k):
            keep = jnp.where(k < modes[s], 1.0, 0.0).astype(F32)
            tk[k, s:s + 1, :] = traces[s, k:k + 1, :] * keep
    for k in range(n_k):
        for b in range(n_b):
            planes[k, pl.ds(b, n_s, stride=n_b), :] = rows_of(tk[k], b)
    mine = jnp.where(wide == tile + lax.broadcasted_iota(jnp.int32, (n_s, LANES), 0), 1.0, 0.0).astype(F32)
    for b in range(n_b):
        planes[n_k, pl.ds(b, n_s, stride=n_b), :] = mine

    def pick_planes(n, carry):
        for side in range(2):
            for m in range(8):
                at = jnp.maximum(sends[side, n * 8 + m], 0)
                for k in range(n_k + 1):
                    tmsg[side, k, pl.ds(n * 8 + m, 1), :] = planes[k, pl.ds(at, 1), :]
        return carry
    lax.fori_loop(0, slots // 8, pick_planes, 0)
    fetch[6].wait()
    jump_start(rhs, 0)

    pl.semaphore_wait(barrier, n_sub - 1 + n_crs - 1)

    sub_start(0, col, ())
    factor_copies = both((factor, factor), wrecv, w_send, w_recv)
    trace_copies = both((tmsg.at[0], tmsg.at[1]), trecv, t_send, t_recv)
    for one in factor_copies + jump_copies(0) + trace_copies:
        one.start()

    for one in factor_copies:
        one.wait_recv()
    for side in range(2):
        for s in range(n_s):
            for k in range(n_k):
                wk[2 * side, k, s:s + 1, :] = wrecv[side, s * n_k + k:s * n_k + k + 1, :]
    jres[...] = jump_end(rhs[...], 0)
    res[...] = rhs[...]
    member[...] = jnp.zeros(member.shape, F32)
    inner[...] = jnp.zeros(inner.shape, F32)
    col, _ = sub_end(0)
    back(0, col)

    for one in trace_copies:
        one.wait_recv()
    for side in range(2):
        for k in range(n_k):
            planes[k, pl.ds(n_local + side * slots, slots), :] = trecv[side, k]
        planes[n_k, pl.ds(n_local + side * slots, slots), :] = pltpu.roll(
            trecv[side, n_k], LANES - tile if side == 0 else tile, 1)

    def pair_planes(s, carry):
        for b in range(n_b):
            code = partner[s, b]
            at = jnp.maximum(code, 0)
            keep = jnp.where(code < 0, 0.0, 1.0).astype(F32)
            for k in range(n_k + 1):
                mates[k, pl.ds(s * n_b + b, 1), :] = planes[k, pl.ds(at, 1), :] * keep
        return carry
    lax.fori_loop(0, n_s, pair_planes, 0)
    for b in range(n_b):
        hot = mates[n_k, pl.ds(b, n_s, stride=n_b), :]
        member[b * tile:b * tile + n_s, :] = hot
        linked = lane_sum(hot)
        for k in range(n_k):
            tp[k, :, b * LANES:(b + 1) * LANES] = mates[k, pl.ds(b, n_s, stride=n_b), :]
            tl[k, :, b * LANES:(b + 1) * LANES] = rows_of(tk[k], b) * linked
    turned = jnp.concatenate([jnp.transpose(member[0:LANES, :]), jnp.transpose(
        jnp.concatenate([member[LANES:, :], jnp.zeros((2 * LANES - member.shape[0], LANES), F32)], axis=0))], axis=1)
    member_t[...] = turned[:3 * tile, :]
    start_col = restrict_col(jres[...])

    mix, _ = back_end(0)
    expand(mix)
    fetch[7].wait()
    out_m[...] = lift[...]
    multiply(2.0 * lift[...], 0)
    sub_start(1, start_col - 2.0 * adjoint_col(qv[...]), ())
    jump_start(qv, 1)
    for one in jump_copies(1):
        one.start()
    applied = jump_end(qv[...], 1)
    r = res[...] - applied
    res[...] = r
    jres[...] = jres[...] - 2.0 * applied
    square_start(0, r)
    col, _ = sub_end(1)
    back(1, col)
    mix, folded = back_end(1)
    expand(mix)
    rw = square_end(0) - folded
    way[...] = res[...] - lift[...]
    jway[...] = jres[...] - 2.0 * lift[...]
    for turn in range(ITERATIONS):
        final = turn == ITERATIONS - 1
        multiply(jway[...], 1 + turn)
        q = qv[...]
        sub_start(2 + turn, 2.0 * adjoint_col(q), (total(jway[...] * q),))
        jump_start(qv, 2 + turn)
        for one in jump_copies(2 + turn):
            one.start()
        applied = jump_end(qv[...], 2 + turn)
        qv[...] = applied
        change, tail = sub_end(2 + turn)
        alpha = rw / tail[:, 0:1]
        col = col - alpha * change
        back(2 + turn, col)
        r = res[...] - alpha * qv[...]
        res[...] = r
        if not final:
            square_start(1 + turn, r)
            jres[...] = jres[...] - 2.0 * alpha * qv[...]
        out_m[...] = out_m[...] + alpha * way[...]
        mix, folded = back_end(2 + turn)
        expand(mix)
        if final:
            out_p[...] = res[...] - lift[...]
        else:
            following = square_end(1 + turn) - folded
            beta = following / rw
            jway[...] = jres[...] - 2.0 * lift[...] + beta * jway[...]
            way[...] = res[...] - lift[...] + beta * way[...]
            rw = following

    for n in range(ITERATIONS + 2):
        arrivals(crecv.at[n], c_send.at[n], c_recv.at[n], "sub", sub, n_sub).wait_send()
        arrivals(xrecv.at[n], x_send.at[n], x_recv.at[n], "crs", crs, n_crs).wait_send()
    for n in range(ITERATIONS + 1):
        arrivals(qrecv.at[n], q_send.at[n], q_recv.at[n], "crs", crs, n_crs).wait_send()
    for n in range(ITERATIONS):
        arrivals(rrecv.at[n], r_send.at[n], r_recv.at[n], "sub", sub, n_sub).wait_send()
    for j in range(ITERATIONS + 2):
        for one in jump_copies(j):
            one.wait_send()
    for one in factor_copies + trace_copies:
        one.wait_send()


def local(n_sub, n_crs, ops, traces, factor, partner, sends, modes, rhs, load):
    n_s, n_row, order = ops.shape
    n_k = traces.shape[1]
    n_col = factor.shape[1]
    slots = sends.shape[1]
    n_b = order // LANES
    n_local = n_s * n_b
    n_c, n_q, n_j, n_r = ITERATIONS + 2, ITERATIONS + 1, ITERATIONS + 2, ITERATIONS
    far = pl.BlockSpec(memory_space=pltpu.HBM)
    vmem = pl.BlockSpec(memory_space=pltpu.VMEM)
    dma = pltpu.SemaphoreType.DMA
    vector = (n_s, order)
    small = (partner, sends, modes, load)
    large = (ops, traces, factor, rhs)
    shapes = [
        (n_k, n_s, order),
        (n_k, n_s, order),
        (n_k, n_s, order),
        (3, n_k, n_s, n_col),
        (n_k + 1, n_local + 2 * slots, LANES),
        (n_k + 1, n_local, LANES),
        (n_b * 16, LANES),
        (48, 2 * LANES),
        (2 * LANES, LANES),
        (n_local + 2 * slots, LANES),
        (n_local, LANES),
        vector,
        vector,
        vector,
        vector,
        vector,
        vector,
        (n_c, 4, LANES),
        (n_c, n_sub, 4, LANES),
        (n_c, 8, LANES),
        (n_c, n_crs, 8, LANES),
        (n_q, 2, n_s, LANES),
        (n_q, n_crs, 2, n_s, LANES),
        (n_j, 2, slots, LANES),
        (n_j, 2, slots, LANES),
        (2, n_k + 1, slots, LANES),
        (2, n_k + 1, slots, LANES),
        (2,) + factor.shape,
        (n_r, 1, LANES),
        (n_r, n_sub, 1, LANES),
    ]
    sems = [(8,), (n_c,), (n_c,), (n_c,), (n_c,), (n_q,), (n_q,), (n_j, 2), (n_j, 2), (2,), (2,), (2,), (2,),
            (n_r,), (n_r,)]
    return pl.pallas_call(
        functools.partial(kernel, n_sub, n_crs),
        out_shape=(jax.ShapeDtypeStruct(vector, F32), jax.ShapeDtypeStruct(vector, F32)),
        in_specs=[far] * 8,
        out_specs=(vmem, vmem),
        scratch_shapes=(
            [pltpu.SMEM(a.shape, a.dtype) for a in small]
            + [pltpu.VMEM(a.shape, a.dtype) for a in large]
            + [pltpu.VMEM(a, F32) for a in shapes]
            + [dma(a) for a in sems]
        ),
        compiler_params=pltpu.CompilerParams(
            collective_id=0, has_side_effects=True, vmem_limit_bytes=67043328
        ),
    )(*small, *large)


def solution(mesh):
    return jax.shard_map(
        functools.partial(local, mesh.shape["sub"], mesh.shape["crs"]),
        mesh=mesh,
        in_specs=(
            P("sub", "crs", None),
            P("sub", None, None),
            P("sub", "crs"),
            P("sub", None),
            P("sub", None),
            P("sub"),
            P("sub", None),
            P("sub"),
        ),
        out_specs=(P("sub", None), P("sub", None)),
        check_vma=False,
    )
```

```python
import functools

import jax
import jax.numpy as jnp
from jax import lax
from jax.experimental import pallas as pl
from jax.experimental.pallas import tpu as pltpu
from jax.sharding import PartitionSpec as P

ITERATIONS = 2
LANES = 128
F32 = jnp.float32


def lane_sum(a):
    return jnp.sum(a, axis=1, keepdims=True)


def total(a):
    return jnp.sum(lane_sum(a), axis=0, keepdims=True)


def kernel(
    n_sub, n_crs,
    partner_in, sends_in, modes_in, load_in, ops_in, traces_in, factor_in, rhs_in,
    out_m, out_p,
    partner, sends, modes, load, ops, traces, factor, rhs,
    tl, tp, wk, planes, mates, member, member_t, inner, mates_x, gather, mate, lift, qv, applied, res, jres, way, jway, mult,
    rounded, cols, lines, col_now, extra, rw, chunk,
    cmsg, crecv, xmsg, xrecv, qmsg, qrecv, hmsg, hrecv, tmsg, trecv, wrecv, rmsg, rrecv,
    in_sem, c_send, c_recv, x_send, x_recv, q_send, q_recv, h_send, h_recv, t_send, t_recv, w_send, w_recv,
    r_send, r_recv,
):
    n_s, n_row, order = ops.shape
    n_b = order // LANES
    n_local = n_s * n_b
    n_k = tl.shape[0]
    last = ITERATIONS + 1
    n_col = factor.shape[1]
    slots = sends.shape[1]
    tile = 16
    sub = lax.axis_index("sub")
    crs = lax.axis_index("crs")

    pairs = ((partner_in, partner), (sends_in, sends), (modes_in, modes), (load_in, load),
             (factor_in, factor), (traces_in, traces), (rhs_in, rhs), (ops_in, ops))
    fetch = [pltpu.make_async_copy(a, b, in_sem.at[n]) for n, (a, b) in enumerate(pairs)]
    for one in fetch:
        one.start()

    barrier = pltpu.get_barrier_semaphore()

    def greet(axis, me, count):
        def one(t, carry):
            pl.semaphore_signal(
                barrier, inc=1, device_id={axis: lax.rem(me + t, count)},
                device_id_type=pl.DeviceIdType.MESH,
            )
            return carry
        lax.fori_loop(1, count, one, 0)

    greet("sub", sub, n_sub)
    greet("crs", crs, n_crs)

    def copy(src, dst, send, recv, where):
        return pltpu.make_async_remote_copy(
            src_ref=src, dst_ref=dst, send_sem=send, recv_sem=recv,
            device_id=where, device_id_type=pl.DeviceIdType.MESH,
        )

    def spread(msg, slots_ref, send, recv, axis, me, count):
        def one(t, carry):
            copy(msg, slots_ref.at[t - 1], send, recv, {axis: lax.rem(me + t, count)}).start()
            return carry
        lax.fori_loop(1, count, one, 0)

    def arrivals(slots_ref, send, recv, axis, me, count):
        whole = slots_ref.at[pl.ds(0, count - 1)]
        return copy(whole, whole, send, recv, {axis: lax.rem(me + 1, count)})

    def slot_of(who, me, count):
        return lax.rem(me - who - 1 + count, count)

    before, after = lax.rem(sub + n_sub - 1, n_sub), lax.rem(sub + 1, n_sub)

    def both(msg, recv_ref, send, recv):
        return [copy(msg[0], recv_ref.at[1], send.at[0], recv.at[1], {"sub": before}),
                copy(msg[1], recv_ref.at[0], send.at[1], recv.at[0], {"sub": after})]

    def rows_of(v, b):
        return v[:, b * LANES:(b + 1) * LANES]

    def jump_start(v, j):
        for b in range(n_b):
            gather[pl.ds(b, n_s, stride=n_b), :] = v[b]

        def pick(n, carry):
            for side in range(2):
                for m in range(8):
                    at = jnp.maximum(sends[side, n * 8 + m], 0)
                    hmsg[j, side, pl.ds(n * 8 + m, 1), :] = gather[pl.ds(at, 1), :]
            return carry
        lax.fori_loop(0, slots // 8, pick, 0)

    def jump_copies(j):
        return both((hmsg.at[j, 0], hmsg.at[j, 1]), hrecv.at[j], h_send.at[j], h_recv.at[j])

    def jump_end(v, out, j):
        one, two = jump_copies(j)
        one.wait_recv()
        two.wait_recv()
        for side in range(2):
            gather[pl.ds(n_local + side * slots, slots), :] = hrecv[j, side]

        def pair(s, carry):
            for b in range(n_b):
                code = partner[s, b]
                at = jnp.where(code < 0, s * n_b + b, code)
                mate[pl.ds(s * n_b + b, 1), :] = gather[pl.ds(at, 1), :]
            return carry
        lax.fori_loop(0, n_s, pair, 0)
        for b in range(n_b):
            out[b] = v[b] - mate[pl.ds(b, n_s, stride=n_b), :]

    lane = lax.broadcasted_iota(jnp.int32, (1, LANES), 1)
    wide = lax.broadcasted_iota(jnp.int32, (n_s, LANES), 1)

    def sub_start(n, col, scalars):
        rows = []
        for at in range(3):
            piece = col[:, at * LANES:min((at + 1) * LANES, n_col)]
            if piece.shape[1] < LANES:
                piece = jnp.concatenate([piece, jnp.zeros((1, LANES - piece.shape[1]), F32)], axis=1)
            rows.append(piece)
        last = jnp.zeros((1, LANES), F32)
        for at, value in enumerate(scalars):
            last = jnp.where(lane == at, value, last)
        msg = jnp.concatenate(rows + [last], axis=0)
        cmsg[n] = msg
        spread(cmsg.at[n], crecv.at[n], c_send.at[n], c_recv.at[n], "sub", sub, n_sub)

    def tree(got):
        while len(got) > 1:
            got = [got[i] + got[i + 1] for i in range(0, len(got), 2)]
        return got[0]

    def sub_end(n):
        arrivals(crecv.at[n], c_send.at[n], c_recv.at[n], "sub", sub, n_sub).wait_recv()
        tot = tree([crecv[n, at] for at in range(n_sub - 1)] + [cmsg[n]])
        col = jnp.concatenate([tot[0:1], tot[1:2], tot[2:3, :n_col - 2 * LANES]], axis=1)
        return col, tot[3:4]

    def square_start(n, v):
        line = jnp.where(lane == 0, total(jnp.sum(v * v, axis=0)), 0.0)
        rmsg[n] = line
        spread(rmsg.at[n], rrecv.at[n], r_send.at[n], r_recv.at[n], "sub", sub, n_sub)

    def square_end(n):
        arrivals(rrecv.at[n], r_send.at[n], r_recv.at[n], "sub", sub, n_sub).wait_recv()
        return tree([rrecv[n, at] for at in range(n_sub - 1)] + [rmsg[n]])[:, 0:1]

    n_x = 3 * n_k
    fold_at = 2 * n_x + 4

    def back(n, col):
        mix = jnp.zeros((n_s, LANES), F32)
        for near in range(3):
            for k in range(n_k):
                mix = jnp.where(wide == near * n_k + k, lane_sum(wk[near, k] * col), mix)
        low = jnp.concatenate([mix[8:n_s], jnp.zeros((16 - n_s, LANES), F32)], axis=0)
        msg = mix[0:8] + pltpu.roll(low, n_x, 1)
        at = (lax.broadcasted_iota(jnp.int32, (8, LANES), 1) == fold_at) & (
            lax.broadcasted_iota(jnp.int32, (8, LANES), 0) == 0)
        msg = jnp.where(at, lane_sum(col * col), msg)
        xmsg[n] = msg
        xrecv[n, n_crs - 1] = msg
        spread(xmsg.at[n], xrecv.at[n], x_send.at[n], x_recv.at[n], "crs", crs, n_crs)

    def back_end(n):
        arrivals(xrecv.at[n], x_send.at[n], x_recv.at[n], "crs", crs, n_crs).wait_recv()
        tot = tree([xrecv[n, slot_of(who, crs, n_crs)] for who in range(n_crs)])
        low = pltpu.roll(tot, LANES - n_x, 1)
        return jnp.concatenate([tot, low[:n_s - 8]], axis=0), tot[0:1, fold_at:fold_at + 1]

    def expand(mix):
        spare = jnp.zeros((tile - n_s, LANES), F32)
        rows = []
        for near in range(3):
            rows += [pltpu.roll(mix, LANES - near * n_k, 1) if near else mix, spare]
        rows.append(jnp.zeros((LANES - 3 * tile, LANES), F32))
        far = jnp.dot(member[...].reshape(n_b * tile, LANES), jnp.concatenate(rows, axis=0),
                      precision=lax.Precision.HIGHEST, preferred_element_type=F32)
        mates_x[...] = far.reshape(n_b, tile, LANES)
        own = [jnp.broadcast_to(mix[:, n_k + k:n_k + k + 1], (n_s, LANES)) for k in range(n_k)]

        def step(g, carry):
            for i in range(4):
                b = g * 4 + i
                theirs = mates_x[b][:n_s]
                acc = None
                for k in range(n_k):
                    term = tl[k, b] * own[k] - tp[k, b] * theirs[:, k:k + 1]
                    acc = term if acc is None else acc + term
                lift[b] = acc
            return carry
        lax.fori_loop(0, n_b // 4, step, 0)

    def restrict_col(jv):
        acc = None
        for k in range(n_k):
            term = wk[1, k] * lane_sum(jnp.sum(tl[k] * jv, axis=0))
            acc = term if acc is None else acc + term
        return jnp.sum(acc, axis=0, keepdims=True)

    def adjoint_col():
        def step(g, own):
            own = list(own)
            for i in range(4):
                b = g * 4 + i
                q = qv[b]
                line = jnp.zeros((n_s, LANES), F32)
                for k in range(n_k):
                    line = jnp.where(wide == k, lane_sum(tp[k, b] * q), line)
                    own[k] = own[k] + tl[k, b] * q
                inner[b, 0:n_s, :] = line
            return tuple(own)
        own = lax.fori_loop(0, n_b // 4, step, tuple(jnp.zeros((n_s, LANES), F32) for k in range(n_k)))
        away = jnp.dot(member_t[...], inner[...].reshape(2 * LANES, LANES), precision=lax.Precision.HIGHEST,
                       preferred_element_type=F32)
        acc = None
        for k in range(n_k):
            for near in range(3):
                weight = -away[near * tile:near * tile + n_s, k:k + 1]
                if near == 1:
                    weight = weight + lane_sum(own[k])
                term = wk[near, k] * weight
                acc = term if acc is None else acc + term
        return jnp.sum(acc, axis=0, keepdims=True)

    odd = lax.rem(crs, 2) == 1
    n_mx = n_s // 3
    here = lax.broadcasted_iota(jnp.int32, (n_row, LANES), 1)

    def multiply(n):
        rounded[...] = jway[...].astype(jnp.bfloat16).astype(F32)

        def step(i, carry):
            line = jnp.concatenate([rounded[b, pl.ds(i, 1), :] for b in range(n_b)], axis=1)
            out = lax.dot_general(jnp.broadcast_to(line, (16, order)).astype(jnp.bfloat16), ops[i],
                                  (((1,), (1,)), ((), ())), preferred_element_type=F32)
            lines[0, pl.ds(i, 1), :] = out[0:1, :LANES]
            lines[1, pl.ds(i, 1), :] = jnp.concatenate(
                [out[0:1, LANES:], jnp.zeros((1, 2 * LANES - n_row), F32)], axis=1)
            for j in range(2):
                s = n_mx + 2 * i + j
                acc = None
                for b in range(n_b):
                    term = ops[s, :, b * LANES:(b + 1) * LANES].astype(F32) * rounded[b, pl.ds(s, 1), :]
                    acc = term if acc is None else acc + term
                cols[0:n_row, :] = jnp.where(here == s, lane_sum(acc), cols[0:n_row, :])
            return carry
        lax.fori_loop(0, n_mx, step, 0)
        top = lax.broadcasted_iota(jnp.int32, (n_s, LANES), 0) < n_mx
        acc = jnp.concatenate([
            jnp.where(top, lines[half], jnp.transpose(cols[half * LANES:(half + 1) * LANES, :])[:n_s])
            for half in range(2)], axis=1)[:, :n_row]
        blank = jnp.zeros((n_s, 2 * LANES - n_row), F32)
        lined = jnp.where(odd, jnp.concatenate([blank, acc], axis=1), jnp.concatenate([acc, blank], axis=1))
        for half in range(2):
            piece = rows_of(lined, half)
            qmsg[n, half] = piece
            qrecv[n, n_crs - 1, half] = piece
        spread(qmsg.at[n], qrecv.at[n], q_send.at[n], q_recv.at[n], "crs", crs, n_crs)
        arrivals(qrecv.at[n], q_send.at[n], q_recv.at[n], "crs", crs, n_crs).wait_recv()
        for pair in range(n_crs // 2):
            even, uneven = slot_of(2 * pair, crs, n_crs), slot_of(2 * pair + 1, crs, n_crs)
            qv[3 * pair] = qrecv[n, even, 0]
            qv[3 * pair + 1] = jnp.where(wide < LANES // 2, qrecv[n, even, 1], qrecv[n, uneven, 0])
            qv[3 * pair + 2] = qrecv[n, uneven, 1]

    for one in fetch[:5]:
        one.wait()
    def by_mode(near, rows_in):
        for at in range(3):
            piece = rows_in[:, at * LANES:min((at + 1) * LANES, n_col)]
            chunk[at, :, 0:piece.shape[1]] = piece
        for k in range(n_k):
            for at in range(3):
                wide_at = min((at + 1) * LANES, n_col) - at * LANES
                wk[near, k, :, at * LANES:at * LANES + wide_at] = chunk[at, pl.ds(k, n_s, stride=n_k), :][:, :wide_at]
    by_mode(1, factor)
    depth = lax.broadcasted_iota(jnp.int32, (n_s, LANES), 0)

    def take_load(s, acc):
        line = jnp.zeros((1, LANES), F32)
        for k in range(n_k):
            line = jnp.where(lane == k, jnp.where(k < modes[s], load[s * n_k + k], 0.0), line)
        return jnp.where(depth == s, line, acc)
    loaded = lax.fori_loop(0, n_s, take_load, jnp.zeros((n_s, LANES), F32))
    acc = None
    for k in range(n_k):
        term = wk[1, k] * loaded[:, k:k + 1]
        acc = term if acc is None else acc + term
    first_col = jnp.sum(acc, axis=0, keepdims=True)
    fetch[5].wait()

    def place(s, carry):
        for k in range(n_k):
            keep = jnp.where(k < modes[s], 1.0, 0.0).astype(F32)
            for b in range(n_b):
                planes[k, pl.ds(s * n_b + b, 1), :] = traces[s, k:k + 1, b * LANES:(b + 1) * LANES] * keep
        return carry
    lax.fori_loop(0, n_s, place, 0)
    mine = jnp.where(wide == tile + depth, 1.0, 0.0).astype(F32)
    for b in range(n_b):
        planes[n_k, pl.ds(b, n_s, stride=n_b), :] = mine

    def pick_planes(n, carry):
        for side in range(2):
            for m in range(4):
                at = jnp.maximum(sends[side, n * 4 + m], 0)
                for k in range(n_k + 1):
                    tmsg[side, k, pl.ds(n * 4 + m, 1), :] = planes[k, pl.ds(at, 1), :]
        return carry
    lax.fori_loop(0, slots // 4, pick_planes, 0)
    fetch[6].wait()
    for b in range(n_b):
        res[b] = rhs[:, b * LANES:(b + 1) * LANES]
    jump_start(res, 0)

    pl.semaphore_wait(barrier, n_sub - 1 + n_crs - 1)

    sub_start(0, -first_col, ())
    factor_copies = both((factor, factor), wrecv, w_send, w_recv)
    trace_copies = both((tmsg.at[0], tmsg.at[1]), trecv, t_send, t_recv)
    for one in factor_copies + jump_copies(0) + trace_copies:
        one.start()

    for ref in (member, inner, cols, mult, way, jway, applied, col_now, extra, rw):
        ref[...] = jnp.zeros(ref.shape, F32)
    for one in factor_copies:
        one.wait_recv()
    for side in range(2):
        by_mode(2 * side, wrecv.at[side])
    jump_end(res, jres, 0)
    fetch[7].wait()

    def take_traces():
        for one in trace_copies:
            one.wait_recv()
        for side in range(2):
            for k in range(n_k):
                planes[k, pl.ds(n_local + side * slots, slots), :] = trecv[side, k]
            planes[n_k, pl.ds(n_local + side * slots, slots), :] = pltpu.roll(
                trecv[side, n_k], LANES - tile if side == 0 else tile, 1)

        def pair_planes(s, carry):
            for b in range(n_b):
                code = partner[s, b]
                at = jnp.maximum(code, 0)
                keep = jnp.where(code < 0, 0.0, 1.0).astype(F32)
                for k in range(n_k + 1):
                    mates[k, pl.ds(s * n_b + b, 1), :] = planes[k, pl.ds(at, 1), :] * keep
            return carry
        lax.fori_loop(0, n_s, pair_planes, 0)
        for b in range(n_b):
            hot = mates[n_k, pl.ds(b, n_s, stride=n_b), :]
            member[b, 0:n_s, :] = hot
            linked = lane_sum(hot)
            for k in range(n_k):
                tp[k, b] = mates[k, pl.ds(b, n_s, stride=n_b), :]
                tl[k, b] = planes[k, pl.ds(b, n_s, stride=n_b), :] * linked
        flat = member[...].reshape(n_b * tile, LANES)
        turned = jnp.concatenate([jnp.transpose(flat[:LANES]), jnp.transpose(jnp.concatenate(
            [flat[LANES:], jnp.zeros((2 * LANES - n_b * tile, LANES), F32)], axis=0))], axis=1)
        member_t[...] = turned[:3 * tile, :]
        extra[...] = restrict_col(jres[...])

    def phase(n, carry):
        fresh = n <= 1
        change, tail = sub_end(n)
        alpha = jnp.where(fresh, jnp.ones((1, 1), F32), rw[:, 0:1] / jnp.where(fresh, jnp.ones((1, 1), F32), tail[:, 0:1]))
        col = jnp.where(fresh, jnp.zeros(change.shape, F32), col_now[...]) - alpha * change
        col_now[...] = col
        back(n, col)
        r = res[...] - alpha * applied[...]
        res[...] = r

        @pl.when((n >= 1) & (n < last))
        def _():
            square_start(n - 1, res[...])
            jres[...] = jres[...] - 2.0 * alpha * applied[...]

        @pl.when(n == 0)
        def _():
            take_traces()

        @pl.when(n > 1)
        def _():
            mult[...] = mult[...] + alpha * way[...]
        mix, folded = back_end(n)
        expand(mix)

        @pl.when(n == 0)
        def _():
            mult[...] = lift[...]
            jway[...] = 2.0 * lift[...]

        @pl.when((n >= 1) & (n < last))
        def _():
            following = square_end(n - 1) - folded
            beta = jnp.where(fresh, jnp.zeros((1, 1), F32), following / jnp.where(fresh, jnp.ones((1, 1), F32), rw[:, 0:1]))
            jway[...] = jres[...] - 2.0 * lift[...] + jnp.where(fresh, 0.0, beta * jway[...])
            way[...] = res[...] - lift[...] + beta * way[...]
            rw[...] = jnp.broadcast_to(following, rw.shape)

        @pl.when(n < last)
        def _():
            multiply(n)
            message = 2.0 * adjoint_col() - extra[...]
            sub_start(n + 1, message, (total(jnp.sum(jway[...] * qv[...], axis=0)),))
            jump_start(qv, n + 1)
            for one in jump_copies(n + 1):
                one.start()
            extra[...] = jnp.zeros(extra.shape, F32)
            jump_end(qv, applied, n + 1)
        return carry
    lax.fori_loop(0, last + 1, phase, 0)

    for b in range(n_b):
        out_m[:, b * LANES:(b + 1) * LANES] = mult[b]
        out_p[:, b * LANES:(b + 1) * LANES] = res[b] - lift[b]

    for n in range(ITERATIONS + 2):
        arrivals(crecv.at[n], c_send.at[n], c_recv.at[n], "sub", sub, n_sub).wait_send()
        arrivals(xrecv.at[n], x_send.at[n], x_recv.at[n], "crs", crs, n_crs).wait_send()
    for n in range(ITERATIONS + 1):
        arrivals(qrecv.at[n], q_send.at[n], q_recv.at[n], "crs", crs, n_crs).wait_send()
    for n in range(ITERATIONS):
        arrivals(rrecv.at[n], r_send.at[n], r_recv.at[n], "sub", sub, n_sub).wait_send()
    for j in range(ITERATIONS + 2):
        for one in jump_copies(j):
            one.wait_send()
    for one in factor_copies + trace_copies:
        one.wait_send()


def local(n_sub, n_crs, ops, traces, factor, partner, sends, modes, rhs, load):
    n_s, n_row, order = ops.shape
    n_k = traces.shape[1]
    n_col = factor.shape[1]
    slots = sends.shape[1]
    n_b = order // LANES
    n_local = n_s * n_b
    n_c, n_q, n_j, n_r = ITERATIONS + 2, ITERATIONS + 1, ITERATIONS + 2, ITERATIONS
    far = pl.BlockSpec(memory_space=pltpu.HBM)
    vmem = pl.BlockSpec(memory_space=pltpu.VMEM)
    dma = pltpu.SemaphoreType.DMA
    vector = (n_b, n_s, LANES)
    small = (partner, sends, modes, load)
    large = (ops, traces, factor, rhs)
    shapes = [
        (n_k,) + vector,
        (n_k,) + vector,
        (3, n_k, n_s, n_col),
        (n_k + 1, n_local + 2 * slots, LANES),
        (n_k + 1, n_local, LANES),
        (n_b, 16, LANES),
        (48, 2 * LANES),
        (16, 16, LANES),
        (n_b, 16, LANES),
        (n_local + 2 * slots, LANES),
        (n_local, LANES),
        vector,
        vector,
        vector,
        vector,
        vector,
        vector,
        vector,
        vector,
        vector,
        (2 * LANES, LANES),
        (2, n_s, LANES),
        (1, n_col),
        (1, n_col),
        (1, LANES),
        (3, n_s * n_k, LANES),
        (n_c, 4, LANES),
        (n_c, n_sub - 1, 4, LANES),
        (n_c, 8, LANES),
        (n_c, n_crs, 8, LANES),
        (n_q, 2, n_s, LANES),
        (n_q, n_crs, 2, n_s, LANES),
        (n_j, 2, slots, LANES),
        (n_j, 2, slots, LANES),
        (2, n_k + 1, slots, LANES),
        (2, n_k + 1, slots, LANES),
        (2,) + factor.shape,
        (n_r, 1, LANES),
        (n_r, n_sub - 1, 1, LANES),
    ]
    sems = [(8,), (n_c,), (n_c,), (n_c,), (n_c,), (n_q,), (n_q,), (n_j, 2), (n_j, 2), (2,), (2,), (2,), (2,),
            (n_r,), (n_r,)]
    return pl.pallas_call(
        functools.partial(kernel, n_sub, n_crs),
        out_shape=(jax.ShapeDtypeStruct((n_s, order), F32), jax.ShapeDtypeStruct((n_s, order), F32)),
        in_specs=[far] * 8,
        out_specs=(vmem, vmem),
        scratch_shapes=(
            [pltpu.SMEM(a.shape, a.dtype) for a in small]
            + [pltpu.VMEM(a.shape, a.dtype) for a in large]
            + [pltpu.VMEM(a, F32) for a in shapes]
            + [dma(a) for a in sems]
        ),
        compiler_params=pltpu.CompilerParams(
            collective_id=0, has_side_effects=True, vmem_limit_bytes=40 * 1024 * 1024
        ),
    )(*[pltpu.with_memory_space_constraint(a, pltpu.HBM) for a in small + large])


def solution(mesh):
    return jax.shard_map(
        functools.partial(local, mesh.shape["sub"], mesh.shape["crs"]),
        mesh=mesh,
        in_specs=(
            P("sub", "crs", None),
            P("sub", None, None),
            P("sub", "crs"),
            P("sub", None),
            P("sub", None),
            P("sub"),
            P("sub", None),
            P("sub"),
        ),
        out_specs=(P("sub", None), P("sub", None)),
        check_vma=False,
    )
```

```python
import functools

import jax
import jax.numpy as jnp
from jax import lax
from jax.experimental import pallas as pl
from jax.experimental.pallas import tpu as pltpu
from jax.sharding import PartitionSpec as P

ITERATIONS = 2
LANES = 128
F32 = jnp.float32


def lane_sum(a):
    return jnp.sum(a, axis=1, keepdims=True)


def total(a):
    return jnp.sum(lane_sum(a), axis=0, keepdims=True)


def kernel(
    n_sub, n_crs,
    partner_in, sends_in, modes_in, load_in, ops_in, traces_in, factor_in, rhs_in,
    out_m, out_p,
    partner, sends, modes, load, ops, traces, factor, rhs,
    tl, tp, wk, planes, mates, member, member_t, inner, mates_x, gather, mate, lift, qv, applied, res, jres, way, jway, mult,
    rounded, cols, lines, col_now, extra, rw, chunk,
    cmsg, crecv, xmsg, xrecv, qmsg, qrecv, hmsg, hrecv, tmsg, trecv, wrecv, rmsg, rrecv,
    in_sem, c_send, c_recv, x_send, x_recv, q_send, q_recv, h_send, h_recv, t_send, t_recv, w_send, w_recv,
    r_send, r_recv,
):
    n_s, n_row, order = ops.shape
    n_b = order // LANES
    n_local = n_s * n_b
    n_k = tl.shape[0]
    last = ITERATIONS + 1
    n_col = factor.shape[1]
    slots = sends.shape[1]
    tile = 16
    sub = lax.axis_index("sub")
    crs = lax.axis_index("crs")

    pairs = ((partner_in, partner), (sends_in, sends), (modes_in, modes), (load_in, load),
             (factor_in, factor), (traces_in, traces), (rhs_in, rhs), (ops_in, ops))
    fetch = [pltpu.make_async_copy(a, b, in_sem.at[n]) for n, (a, b) in enumerate(pairs)]
    for one in fetch:
        one.start()

    barrier = pltpu.get_barrier_semaphore()

    def greet(axis, me, count):
        def one(t, carry):
            pl.semaphore_signal(
                barrier, inc=1, device_id={axis: lax.rem(me + t, count)},
                device_id_type=pl.DeviceIdType.MESH,
            )
            return carry
        lax.fori_loop(1, count, one, 0)

    greet("sub", sub, n_sub)
    greet("crs", crs, n_crs)

    def copy(src, dst, send, recv, where):
        return pltpu.make_async_remote_copy(
            src_ref=src, dst_ref=dst, send_sem=send, recv_sem=recv,
            device_id=where, device_id_type=pl.DeviceIdType.MESH,
        )

    def spread(msg, slots_ref, send, recv, axis, me, count):
        def one(t):
            copy(msg, slots_ref.at[t - 1], send, recv, {axis: lax.rem(me + t, count)}).start()
        for t in range(1, count):
            one(t)

    def arrivals(slots_ref, send, recv, axis, me, count):
        whole = slots_ref.at[pl.ds(0, count - 1)]
        return copy(whole, whole, send, recv, {axis: lax.rem(me + 1, count)})

    def slot_of(who, me, count):
        return lax.rem(me - who - 1 + count, count)

    before, after = lax.rem(sub + n_sub - 1, n_sub), lax.rem(sub + 1, n_sub)

    def both(msg, recv_ref, send, recv):
        return [copy(msg[0], recv_ref.at[1], send.at[0], recv.at[1], {"sub": before}),
                copy(msg[1], recv_ref.at[0], send.at[1], recv.at[0], {"sub": after})]

    def rows_of(v, b):
        return v[:, b * LANES:(b + 1) * LANES]

    def jump_start(v, j):
        for b in range(n_b):
            gather[pl.ds(b, n_s, stride=n_b), :] = v[b]

        def pick(n, carry):
            for side in range(2):
                for m in range(8):
                    at = jnp.maximum(sends[side, n * 8 + m], 0)
                    hmsg[j, side, pl.ds(n * 8 + m, 1), :] = gather[pl.ds(at, 1), :]
            return carry
        lax.fori_loop(0, slots // 8, pick, 0)

    def jump_copies(j):
        return both((hmsg.at[j, 0], hmsg.at[j, 1]), hrecv.at[j], h_send.at[j], h_recv.at[j])

    def jump_end(v, out, j):
        one, two = jump_copies(j)
        one.wait_recv()
        two.wait_recv()
        for side in range(2):
            gather[pl.ds(n_local + side * slots, slots), :] = hrecv[j, side]

        def pair(s, carry):
            for b in range(n_b):
                code = partner[s, b]
                at = jnp.where(code < 0, s * n_b + b, code)
                mate[pl.ds(s * n_b + b, 1), :] = gather[pl.ds(at, 1), :]
            return carry
        lax.fori_loop(0, n_s, pair, 0)
        for b in range(n_b):
            out[b] = v[b] - mate[pl.ds(b, n_s, stride=n_b), :]

    lane = lax.broadcasted_iota(jnp.int32, (1, LANES), 1)
    wide = lax.broadcasted_iota(jnp.int32, (n_s, LANES), 1)

    def sub_start(n, col, scalars):
        rows = []
        for at in range(3):
            piece = col[:, at * LANES:min((at + 1) * LANES, n_col)]
            if piece.shape[1] < LANES:
                piece = jnp.concatenate([piece, jnp.zeros((1, LANES - piece.shape[1]), F32)], axis=1)
            rows.append(piece)
        last = jnp.zeros((1, LANES), F32)
        for at, value in enumerate(scalars):
            last = jnp.where(lane == at, value, last)
        msg = jnp.concatenate(rows + [last], axis=0)
        cmsg[n] = msg
        spread(cmsg.at[n], crecv.at[n], c_send.at[n], c_recv.at[n], "sub", sub, n_sub)

    def tree(got):
        while len(got) > 1:
            got = [got[i] + got[i + 1] for i in range(0, len(got), 2)]
        return got[0]

    def sub_end(n):
        arrivals(crecv.at[n], c_send.at[n], c_recv.at[n], "sub", sub, n_sub).wait_recv()
        tot = tree([crecv[n, at] for at in range(n_sub - 1)] + [cmsg[n]])
        col = jnp.concatenate([tot[0:1], tot[1:2], tot[2:3, :n_col - 2 * LANES]], axis=1)
        return col, tot[3:4]

    def square_start(n, v):
        line = jnp.where(lane == 0, total(jnp.sum(v * v, axis=0)), 0.0)
        rmsg[n] = line
        spread(rmsg.at[n], rrecv.at[n], r_send.at[n], r_recv.at[n], "sub", sub, n_sub)

    def square_end(n):
        arrivals(rrecv.at[n], r_send.at[n], r_recv.at[n], "sub", sub, n_sub).wait_recv()
        return tree([rrecv[n, at] for at in range(n_sub - 1)] + [rmsg[n]])[:, 0:1]

    n_x = 3 * n_k
    fold_at = 2 * n_x + 4

    def back(n, col):
        mix = jnp.zeros((n_s, LANES), F32)
        for near in range(3):
            for k in range(n_k):
                mix = jnp.where(wide == near * n_k + k, lane_sum(wk[near, k] * col), mix)
        low = jnp.concatenate([mix[8:n_s], jnp.zeros((16 - n_s, LANES), F32)], axis=0)
        msg = mix[0:8] + pltpu.roll(low, n_x, 1)
        at = (lax.broadcasted_iota(jnp.int32, (8, LANES), 1) == fold_at) & (
            lax.broadcasted_iota(jnp.int32, (8, LANES), 0) == 0)
        msg = jnp.where(at, lane_sum(col * col), msg)
        xmsg[n] = msg
        xrecv[n, n_crs - 1] = msg
        spread(xmsg.at[n], xrecv.at[n], x_send.at[n], x_recv.at[n], "crs", crs, n_crs)

    def back_end(n):
        arrivals(xrecv.at[n], x_send.at[n], x_recv.at[n], "crs", crs, n_crs).wait_recv()
        tot = tree([xrecv[n, slot_of(who, crs, n_crs)] for who in range(n_crs)])
        low = pltpu.roll(tot, LANES - n_x, 1)
        return jnp.concatenate([tot, low[:n_s - 8]], axis=0), tot[0:1, fold_at:fold_at + 1]

    def expand(mix):
        spare = jnp.zeros((tile - n_s, LANES), F32)
        rows = []
        for near in range(3):
            rows += [pltpu.roll(mix, LANES - near * n_k, 1) if near else mix, spare]
        rows.append(jnp.zeros((LANES - 3 * tile, LANES), F32))
        far = jnp.dot(member[...].reshape(n_b * tile, LANES), jnp.concatenate(rows, axis=0),
                      precision=lax.Precision.HIGHEST, preferred_element_type=F32)
        mates_x[...] = far.reshape(n_b, tile, LANES)
        own = [jnp.broadcast_to(mix[:, n_k + k:n_k + k + 1], (n_s, LANES)) for k in range(n_k)]

        def step(g, carry):
            for i in range(4):
                b = g * 4 + i
                theirs = mates_x[b][:n_s]
                acc = None
                for k in range(n_k):
                    term = tl[k, b] * own[k] - tp[k, b] * theirs[:, k:k + 1]
                    acc = term if acc is None else acc + term
                lift[b] = acc
            return carry
        for g in range(n_b // 4):
            step(g, 0)

    def restrict_col(jv):
        acc = None
        for k in range(n_k):
            term = wk[1, k] * lane_sum(jnp.sum(tl[k] * jv, axis=0))
            acc = term if acc is None else acc + term
        return jnp.sum(acc, axis=0, keepdims=True)

    def adjoint_col():
        def step(g, own):
            own = list(own)
            for i in range(4):
                b = g * 4 + i
                q = qv[b]
                line = jnp.zeros((n_s, LANES), F32)
                for k in range(n_k):
                    line = jnp.where(wide == k, lane_sum(tp[k, b] * q), line)
                    own[k] = own[k] + tl[k, b] * q
                inner[b, 0:n_s, :] = line
            return tuple(own)
        own = tuple(jnp.zeros((n_s, LANES), F32) for k in range(n_k))
        for g in range(n_b // 4):
            own = step(g, own)
        away = jnp.dot(member_t[...], inner[...].reshape(2 * LANES, LANES), precision=lax.Precision.HIGHEST,
                       preferred_element_type=F32)
        acc = None
        for k in range(n_k):
            for near in range(3):
                weight = -away[near * tile:near * tile + n_s, k:k + 1]
                if near == 1:
                    weight = weight + lane_sum(own[k])
                term = wk[near, k] * weight
                acc = term if acc is None else acc + term
        return jnp.sum(acc, axis=0, keepdims=True)

    odd = lax.rem(crs, 2) == 1
    n_mx = n_s // 3
    here = lax.broadcasted_iota(jnp.int32, (n_row, LANES), 1)

    def multiply(n):
        rounded[...] = jway[...].astype(jnp.bfloat16).astype(F32)

        def step(i, carry):
            line = jnp.concatenate([rounded[b, pl.ds(i, 1), :] for b in range(n_b)], axis=1)
            out = lax.dot_general(jnp.broadcast_to(line, (16, order)).astype(jnp.bfloat16), ops[i],
                                  (((1,), (1,)), ((), ())), preferred_element_type=F32)
            lines[0, pl.ds(i, 1), :] = out[0:1, :LANES]
            lines[1, pl.ds(i, 1), :] = jnp.concatenate(
                [out[0:1, LANES:], jnp.zeros((1, 2 * LANES - n_row), F32)], axis=1)
            for j in range(2):
                s = n_mx + 2 * i + j
                acc = None
                for b in range(n_b):
                    term = ops[s, :, b * LANES:(b + 1) * LANES].astype(F32) * rounded[b, pl.ds(s, 1), :]
                    acc = term if acc is None else acc + term
                cols[0:n_row, :] = jnp.where(here == s, lane_sum(acc), cols[0:n_row, :])
            return carry
        for i in range(n_mx):
            step(i, 0)
        top = lax.broadcasted_iota(jnp.int32, (n_s, LANES), 0) < n_mx
        acc = jnp.concatenate([
            jnp.where(top, lines[half], jnp.transpose(cols[half * LANES:(half + 1) * LANES, :])[:n_s])
            for half in range(2)], axis=1)[:, :n_row]
        blank = jnp.zeros((n_s, 2 * LANES - n_row), F32)
        lined = jnp.where(odd, jnp.concatenate([blank, acc], axis=1), jnp.concatenate([acc, blank], axis=1))
        for half in range(2):
            piece = rows_of(lined, half)
            qmsg[n, half] = piece
            qrecv[n, n_crs - 1, half] = piece
        spread(qmsg.at[n], qrecv.at[n], q_send.at[n], q_recv.at[n], "crs", crs, n_crs)
        arrivals(qrecv.at[n], q_send.at[n], q_recv.at[n], "crs", crs, n_crs).wait_recv()
        for pair in range(n_crs // 2):
            even, uneven = slot_of(2 * pair, crs, n_crs), slot_of(2 * pair + 1, crs, n_crs)
            qv[3 * pair] = qrecv[n, even, 0]
            qv[3 * pair + 1] = jnp.where(wide < LANES // 2, qrecv[n, even, 1], qrecv[n, uneven, 0])
            qv[3 * pair + 2] = qrecv[n, uneven, 1]

    for one in fetch[:5]:
        one.wait()
    def by_mode(near, rows_in):
        for at in range(3):
            piece = rows_in[:, at * LANES:min((at + 1) * LANES, n_col)]
            chunk[at, :, 0:piece.shape[1]] = piece
        for k in range(n_k):
            for at in range(3):
                wide_at = min((at + 1) * LANES, n_col) - at * LANES
                wk[near, k, :, at * LANES:at * LANES + wide_at] = chunk[at, pl.ds(k, n_s, stride=n_k), :][:, :wide_at]
    by_mode(1, factor)
    depth = lax.broadcasted_iota(jnp.int32, (n_s, LANES), 0)

    def take_load(s, acc):
        line = jnp.zeros((1, LANES), F32)
        for k in range(n_k):
            line = jnp.where(lane == k, jnp.where(k < modes[s], load[s * n_k + k], 0.0), line)
        return jnp.where(depth == s, line, acc)
    loaded = lax.fori_loop(0, n_s, take_load, jnp.zeros((n_s, LANES), F32))
    acc = None
    for k in range(n_k):
        term = wk[1, k] * loaded[:, k:k + 1]
        acc = term if acc is None else acc + term
    first_col = jnp.sum(acc, axis=0, keepdims=True)
    fetch[5].wait()

    def place(s, carry):
        for k in range(n_k):
            keep = jnp.where(k < modes[s], 1.0, 0.0).astype(F32)
            for b in range(n_b):
                planes[k, pl.ds(s * n_b + b, 1), :] = traces[s, k:k + 1, b * LANES:(b + 1) * LANES] * keep
        return carry
    lax.fori_loop(0, n_s, place, 0)
    mine = jnp.where(wide == tile + depth, 1.0, 0.0).astype(F32)
    for b in range(n_b):
        planes[n_k, pl.ds(b, n_s, stride=n_b), :] = mine

    def pick_planes(n, carry):
        for side in range(2):
            for m in range(4):
                at = jnp.maximum(sends[side, n * 4 + m], 0)
                for k in range(n_k + 1):
                    tmsg[side, k, pl.ds(n * 4 + m, 1), :] = planes[k, pl.ds(at, 1), :]
        return carry
    lax.fori_loop(0, slots // 4, pick_planes, 0)
    fetch[6].wait()
    for b in range(n_b):
        res[b] = rhs[:, b * LANES:(b + 1) * LANES]
    jump_start(res, 0)

    pl.semaphore_wait(barrier, n_sub - 1 + n_crs - 1)

    sub_start(0, -first_col, ())
    factor_copies = both((factor, factor), wrecv, w_send, w_recv)
    trace_copies = both((tmsg.at[0], tmsg.at[1]), trecv, t_send, t_recv)
    for one in factor_copies + jump_copies(0) + trace_copies:
        one.start()

    for ref in (member, inner, cols, mult, way, jway, applied, col_now, extra, rw):
        ref[...] = jnp.zeros(ref.shape, F32)
    for one in factor_copies:
        one.wait_recv()
    for side in range(2):
        by_mode(2 * side, wrecv.at[side])
    jump_end(res, jres, 0)
    fetch[7].wait()

    def take_traces():
        for one in trace_copies:
            one.wait_recv()
        for side in range(2):
            for k in range(n_k):
                planes[k, pl.ds(n_local + side * slots, slots), :] = trecv[side, k]
            planes[n_k, pl.ds(n_local + side * slots, slots), :] = pltpu.roll(
                trecv[side, n_k], LANES - tile if side == 0 else tile, 1)

        def pair_planes(s, carry):
            for b in range(n_b):
                code = partner[s, b]
                at = jnp.maximum(code, 0)
                keep = jnp.where(code < 0, 0.0, 1.0).astype(F32)
                for k in range(n_k + 1):
                    mates[k, pl.ds(s * n_b + b, 1), :] = planes[k, pl.ds(at, 1), :] * keep
            return carry
        lax.fori_loop(0, n_s, pair_planes, 0)
        for b in range(n_b):
            hot = mates[n_k, pl.ds(b, n_s, stride=n_b), :]
            member[b, 0:n_s, :] = hot
            linked = lane_sum(hot)
            for k in range(n_k):
                tp[k, b] = mates[k, pl.ds(b, n_s, stride=n_b), :]
                tl[k, b] = planes[k, pl.ds(b, n_s, stride=n_b), :] * linked
        flat = member[...].reshape(n_b * tile, LANES)
        turned = jnp.concatenate([jnp.transpose(flat[:LANES]), jnp.transpose(jnp.concatenate(
            [flat[LANES:], jnp.zeros((2 * LANES - n_b * tile, LANES), F32)], axis=0))], axis=1)
        member_t[...] = turned[:3 * tile, :]
        extra[...] = restrict_col(jres[...])

    def phase(n, carry):
        fresh = n <= 1
        change, tail = sub_end(n)
        alpha = jnp.where(fresh, jnp.ones((1, 1), F32), rw[:, 0:1] / jnp.where(fresh, jnp.ones((1, 1), F32), tail[:, 0:1]))
        col = jnp.where(fresh, jnp.zeros(change.shape, F32), col_now[...]) - alpha * change
        col_now[...] = col
        back(n, col)
        @pl.when(n >= 1)
        def _():
            jump_end(qv, applied, n)
        res[...] = res[...] - alpha * applied[...]

        @pl.when((n >= 1) & (n < last))
        def _():
            square_start(n - 1, res[...])
            jres[...] = jres[...] - 2.0 * alpha * applied[...]

        @pl.when(n == 0)
        def _():
            take_traces()

        @pl.when(n > 1)
        def _():
            mult[...] = mult[...] + alpha * way[...]
        mix, folded = back_end(n)
        expand(mix)

        @pl.when(n == 0)
        def _():
            mult[...] = lift[...]
            jway[...] = 2.0 * lift[...]

        @pl.when((n >= 1) & (n < last))
        def _():
            following = square_end(n - 1) - folded
            beta = jnp.where(fresh, jnp.zeros((1, 1), F32), following / jnp.where(fresh, jnp.ones((1, 1), F32), rw[:, 0:1]))
            jway[...] = jres[...] - 2.0 * lift[...] + jnp.where(fresh, 0.0, beta * jway[...])
            way[...] = res[...] - lift[...] + beta * way[...]
            rw[...] = jnp.broadcast_to(following, rw.shape)

        @pl.when(n < last)
        def _():
            multiply(n)
            message = 2.0 * adjoint_col() - extra[...]
            sub_start(n + 1, message, (total(jnp.sum(jway[...] * qv[...], axis=0)),))
            jump_start(qv, n + 1)
            for one in jump_copies(n + 1):
                one.start()
            extra[...] = jnp.zeros(extra.shape, F32)
        return carry
    lax.fori_loop(0, last + 1, phase, 0)

    for b in range(n_b):
        out_m[:, b * LANES:(b + 1) * LANES] = mult[b]
        out_p[:, b * LANES:(b + 1) * LANES] = res[b] - lift[b]

    for n in range(ITERATIONS + 2):
        arrivals(crecv.at[n], c_send.at[n], c_recv.at[n], "sub", sub, n_sub).wait_send()
        arrivals(xrecv.at[n], x_send.at[n], x_recv.at[n], "crs", crs, n_crs).wait_send()
    for n in range(ITERATIONS + 1):
        arrivals(qrecv.at[n], q_send.at[n], q_recv.at[n], "crs", crs, n_crs).wait_send()
    for n in range(ITERATIONS):
        arrivals(rrecv.at[n], r_send.at[n], r_recv.at[n], "sub", sub, n_sub).wait_send()
    for j in range(ITERATIONS + 2):
        for one in jump_copies(j):
            one.wait_send()
    for one in factor_copies + trace_copies:
        one.wait_send()


def local(n_sub, n_crs, ops, traces, factor, partner, sends, modes, rhs, load):
    n_s, n_row, order = ops.shape
    n_k = traces.shape[1]
    n_col = factor.shape[1]
    slots = sends.shape[1]
    n_b = order // LANES
    n_local = n_s * n_b
    n_c, n_q, n_j, n_r = ITERATIONS + 2, ITERATIONS + 1, ITERATIONS + 2, ITERATIONS
    far = pl.BlockSpec(memory_space=pltpu.HBM)
    vmem = pl.BlockSpec(memory_space=pltpu.VMEM)
    dma = pltpu.SemaphoreType.DMA
    vector = (n_b, n_s, LANES)
    small = (partner, sends, modes, load)
    large = (ops, traces, factor, rhs)
    shapes = [
        (n_k,) + vector,
        (n_k,) + vector,
        (3, n_k, n_s, n_col),
        (n_k + 1, n_local + 2 * slots, LANES),
        (n_k + 1, n_local, LANES),
        (n_b, 16, LANES),
        (48, 2 * LANES),
        (16, 16, LANES),
        (n_b, 16, LANES),
        (n_local + 2 * slots, LANES),
        (n_local, LANES),
        vector,
        vector,
        vector,
        vector,
        vector,
        vector,
        vector,
        vector,
        vector,
        (2 * LANES, LANES),
        (2, n_s, LANES),
        (1, n_col),
        (1, n_col),
        (1, LANES),
        (3, n_s * n_k, LANES),
        (n_c, 4, LANES),
        (n_c, n_sub - 1, 4, LANES),
        (n_c, 8, LANES),
        (n_c, n_crs, 8, LANES),
        (n_q, 2, n_s, LANES),
        (n_q, n_crs, 2, n_s, LANES),
        (n_j, 2, slots, LANES),
        (n_j, 2, slots, LANES),
        (2, n_k + 1, slots, LANES),
        (2, n_k + 1, slots, LANES),
        (2,) + factor.shape,
        (n_r, 1, LANES),
        (n_r, n_sub - 1, 1, LANES),
    ]
    sems = [(8,), (n_c,), (n_c,), (n_c,), (n_c,), (n_q,), (n_q,), (n_j, 2), (n_j, 2), (2,), (2,), (2,), (2,),
            (n_r,), (n_r,)]
    return pl.pallas_call(
        functools.partial(kernel, n_sub, n_crs),
        out_shape=(jax.ShapeDtypeStruct((n_s, order), F32), jax.ShapeDtypeStruct((n_s, order), F32)),
        in_specs=[far] * 8,
        out_specs=(vmem, vmem),
        scratch_shapes=(
            [pltpu.SMEM(a.shape, a.dtype) for a in small]
            + [pltpu.VMEM(a.shape, a.dtype) for a in large]
            + [pltpu.VMEM(a, F32) for a in shapes]
            + [dma(a) for a in sems]
        ),
        compiler_params=pltpu.CompilerParams(
            collective_id=0, has_side_effects=True, vmem_limit_bytes=40 * 1024 * 1024
        ),
    )(*[pltpu.with_memory_space_constraint(a, pltpu.HBM) for a in small + large])


def solution(mesh):
    return jax.shard_map(
        functools.partial(local, mesh.shape["sub"], mesh.shape["crs"]),
        mesh=mesh,
        in_specs=(
            P("sub", "crs", None),
            P("sub", None, None),
            P("sub", "crs"),
            P("sub", None),
            P("sub", None),
            P("sub"),
            P("sub", None),
            P("sub"),
        ),
        out_specs=(P("sub", None), P("sub", None)),
        check_vma=False,
    )
```
